512 devices in a mesh: row: 32 (over z, y_hi, core), col: 16 (over x, y_lo).
Axes of the slice: x: 4, y: 8 (y_hi: 2, y_lo: 4; y = y_hi * 4 + y_lo), z: 8, core: 2. Of those that a mesh axis runs over, the one named last changes fastest.
Arguments:
- rhs_top: bfloat16 [2, 1024, 16384], P(None, 'row', 'col'), may hold values from -6 to 6
- diag_inverse: bfloat16 [2, 1024, 1024], P(None, 'row'), as said below
- panel_coupling: bfloat16 [1024, 1024], P('row'), may hold values from -0.1875 to 0.1875
- trailing_factor: bfloat16 [32768, 2048], P('row', 'col'), may hold values from -0.125 to 0.125
- rhs_trailing: bfloat16 [32768, 16384], P('row', 'col'), may hold values from -6 to 6
Outputs:
- solved: bfloat16 [2, 1024, 16384], P(None, 'row', 'col')
- updated: bfloat16 [32768, 16384], P('row', 'col')
The draws below stay inside these ranges and needn't reach their ends.
Inputs may be any that keep to these rules, and one draw needn't show every extreme that they name: Each diag_inverse[k] is lower triangular.
All inputs are finite; a program needn't handle non-finite values.
Results may differ from the reference program's by a relative error of at most 0.0055.
Values may be sent and summed in bfloat16 or wider, within the bound.
A program may use at most 64 MiB of HBM per device.

```python
import jax
import jax.numpy as jnp
from jax import lax

PB = 1024
ROWS_DEV = 1024
ROWS = 32768
NRHS = 16384


def draw_diag_inverse(key, part):
    key_off, key_diag = jax.random.split(jax.random.fold_in(key, 17))
    rows = lax.broadcasted_iota(jnp.int32, (2, PB, PB), 1)
    cols = lax.broadcasted_iota(jnp.int32, (2, PB, PB), 2)
    off = jax.random.normal(key_off, (2, PB, PB), jnp.float32) * (0.6 * PB ** (-0.5))
    diag = jax.random.uniform(key_diag, (2, PB, PB), jnp.float32, 0.6, 1.4)
    whole = jnp.where(rows > cols, off, jnp.where(rows == cols, diag, jnp.zeros_like(off)))
    return whole.astype(jnp.bfloat16)


def block_scale(key, shape, cuts, smallest, top_value):
    factor_of, own = 1.0, jax.random.fold_in(key, 6)
    for axis_at, blocks in cuts:
        heights = jnp.exp(jax.random.uniform(jax.random.fold_in(own, axis_at), (blocks,), jnp.float32, smallest / len(cuts), top_value / len(cuts)))
        factor_of = factor_of * jnp.repeat(heights, shape[axis_at] // blocks).reshape([-1 if axis == axis_at else 1 for axis in range(len(shape))])
    return factor_of


def bell_draw(key, extent, width, reach, cuts=(), kind=jnp.bfloat16):
    values = jax.random.normal(key, extent, jnp.float32) * width
    if len(cuts) > 0:
        values = block_scale(key, extent, cuts, -0.22, 0.18) * values
    return jnp.clip(values, min=-reach, max=reach).astype(kind)


def setup_inputs(seed: int = 0) -> dict:
    splits = jax.random.split(jax.random.key(seed), 6)
    rhs_top = bell_draw(splits[0], (2, PB, NRHS), 1.0, 6.0, ((1, 32), (2, 16)))
    diag_inverse = draw_diag_inverse(jax.random.fold_in(splits[5], 71), 0)
    panel_coupling = bell_draw(splits[2], (PB, PB), PB ** -0.5, 0.1875, ((0, 32),))
    trailing_factor = bell_draw(splits[3], (ROWS, 2 * PB), (2 * PB) ** -0.5, 0.125, ((0, 32), (1, 16)))
    rhs_trailing = bell_draw(splits[4], (ROWS, NRHS), 1.0, 6.0, ((0, 32), (1, 16)))
    return {"rhs_top": rhs_top, "diag_inverse": diag_inverse, "panel_coupling": panel_coupling, "trailing_factor": trailing_factor, "rhs_trailing": rhs_trailing}


def reference(rhs_top, diag_inverse, panel_coupling, trailing_factor, rhs_trailing):
    first = jnp.dot(diag_inverse[0], rhs_top[0], preferred_element_type=jnp.float32).astype(jnp.bfloat16)
    carried = (rhs_top[1].astype(jnp.float32) - jnp.dot(panel_coupling, first, preferred_element_type=jnp.float32)).astype(jnp.bfloat16)
    second = jnp.dot(diag_inverse[1], carried, preferred_element_type=jnp.float32).astype(jnp.bfloat16)
    solution = jnp.concatenate([first, second], axis=0)
    blocks = ROWS // ROWS_DEV
    factor_blocks = trailing_factor.reshape(blocks, ROWS_DEV, 2 * PB)
    rhs_blocks = rhs_trailing.reshape(blocks, ROWS_DEV, NRHS)

    def update(pair):
        factor_rows, rhs_rows = pair
        product = jnp.dot(factor_rows, solution, preferred_element_type=jnp.float32)
        return (rhs_rows.astype(jnp.float32) - product).astype(jnp.bfloat16)

    updated = lax.map(update, (factor_blocks, rhs_blocks)).reshape(ROWS, NRHS)
    return jnp.stack([first, second]), updated
```

```python
import jax
import jax.numpy as jnp
from jax import lax
from jax.experimental import pallas as pl
from jax.experimental.pallas import tpu as pltpu
from jax.sharding import PartitionSpec as P

MESH = pl.DeviceIdType.MESH
BF = jnp.bfloat16
F32 = jnp.float32

R0, D0, CP, R1, D1 = range(5)
STAGES = ((0, 2), (2, 4), (4, 5))


def kernel(
    rhs_ref, diag_ref, coup_ref, fac_ref, trail_ref,
    solved_ref, upd_ref,
    pan, sol, car, fac, trail, acc, out,
    recv, lrecv, send, lsend, local,
):
    row = lax.axis_index("row")
    col = lax.axis_index("col")
    z, yh, k = row // 4, (row // 2) % 2, row % 2
    x, yl = col // 4, col % 4
    mid = (yl // 2 + yl % 2) % 2 == 1
    sib = row + 1 - 2 * k
    zup, zdn = (row + 4) % 32, (row + 28) % 32
    mate = row + 2 - 4 * yh
    xup, xdn = (col + 4) % 16, (col + 12) % 16
    y1 = x * 4 + yl + 1 - 2 * (yl % 2)
    y2 = x * 4 + 3 - yl

    mine = pl.ds(pl.multiple_of(row * 32, 32), 32)
    loads = [
        pltpu.make_async_copy(rhs_ref.at[0], pan.at[R0, mine, :], local.at[0]),
        pltpu.make_async_copy(diag_ref.at[0], pan.at[D0, mine, :], local.at[1]),
        pltpu.make_async_copy(fac_ref, fac.at[col], local.at[2]),
        pltpu.make_async_copy(coup_ref, pan.at[CP, mine, :], local.at[3]),
        pltpu.make_async_copy(rhs_ref.at[1], pan.at[R1, mine, :], local.at[4]),
        pltpu.make_async_copy(diag_ref.at[1], pan.at[D1, mine, :], local.at[5]),
        pltpu.make_async_copy(trail_ref, trail, local.at[6]),
    ]
    for load in loads:
        load.start()

    barrier = pltpu.get_barrier_semaphore()
    peers = [(sib, col), (zup, col), (zdn, col), (mate, col), (row, xup), (row, xdn), (row, y1)]
    for peer in peers:
        pl.semaphore_signal(barrier, inc=1, device_id=peer, device_id_type=MESH)

    @pl.when(mid)
    def _():
        pl.semaphore_signal(barrier, inc=1, device_id=(row, y2), device_id_type=MESH)
        pl.semaphore_wait(barrier, len(peers) + 1)

    @pl.when(jnp.logical_not(mid))
    def _():
        pl.semaphore_wait(barrier, len(peers))

    sent = []
    later = []
    pushes = [0]

    def block(stage, q):
        low, high = STAGES[stage]
        return pan.at[low:high, pl.ds(pl.multiple_of(q * 32, 32), 32), :]

    def pcopy(stage, q, to, sem):
        return pltpu.make_async_remote_copy(
            src_ref=block(stage, q), dst_ref=block(stage, q),
            send_sem=sem, recv_sem=recv.at[stage, q],
            device_id=(to, col), device_id_type=MESH,
        )

    def push(stage, q, to):
        copy = pcopy(stage, q, to, send.at[pushes[0]])
        pushes[0] += 1
        copy.start()
        sent.append(copy)

    def arrive(stage, q):
        pcopy(stage, q, sib, send.at[0]).wait_recv()

    def rank(zz, j):
        return zz * 4 + (yh + j * (1 - 2 * yh)) * 2 + k

    def own(stage):
        for to in (zup, zdn, mate, sib):
            push(stage, row, to)

    def pair(stage):
        arrive(stage, mate)
        for to in (zup, zdn, sib):
            push(stage, mate, to)

    def hop(stage, h):
        for j in (0, 1):
            if h < 4 or j == 0:
                q = rank((z + 8 - h) % 8, j)
                arrive(stage, q)
                if h < 3 or (h == 3 and j == 0):
                    push(stage, q, zup)
                push(stage, q, sib)
            if h < 4 or j == 1:
                q = rank((z + h) % 8, j)
                arrive(stage, q)
                if h < 3 or (h == 3 and j == 1):
                    push(stage, q, zdn)
                push(stage, q, sib)

    def fill(stage):
        @pl.loop(0, 16)
        def _(i):
            arrive(stage, i * 2 + 1 - k)

    def lcopy(c, to, sem):
        return pltpu.make_async_remote_copy(
            src_ref=fac.at[c], dst_ref=fac.at[c],
            send_sem=sem, recv_sem=lrecv.at[c],
            device_id=(row, to), device_id_type=MESH,
        )

    count = [0]

    def lpush(c, to, wait=True):
        copy = lcopy(c, to, lsend.at[count[0]])
        copy.start()
        if wait:
            sent.append(copy)
        else:
            later.append((c, to, count[0]))
        count[0] += 1

    def larrive(c):
        lcopy(c, xup, lsend.at[0]).wait_recv()

    def lown():
        lpush(col, y1)

        @pl.when(mid)
        def _():
            lpush(col, y2, False)

        lpush(col, xup)
        lpush(col, xdn)

    order = [
        yl + 1 - 2 * (yl % 2),
        2 - yl // 2,
        3 - 3 * (yl // 2),
    ]

    def line(d):
        c = x * 4 + order[d]
        larrive(c)

        @pl.when(mid)
        def _():
            lpush(c, y2 if d == 0 else y1, False)

        lpush(c, xup)
        lpush(c, xdn)

    def ring(m):
        e = [yl, order[0], order[1], order[2]][m]
        below = (x + 3) % 4 * 4 + e
        above = (x + 1) % 4 * 4 + e
        larrive(below)
        if m % 2 == 0:
            lpush(below, xup)
        larrive(above)
        if m % 2 == 1:
            lpush(above, xdn)

    def ringlast():
        for e in (yl, order[0], order[1], order[2]):
            larrive((x + 2) % 4 * 4 + e)

    def first():
        @pl.loop(0, 4)
        def _(n):
            cols = pl.ds(pl.multiple_of(n * 256, 256), 256)
            for i in (0, 1):
                deep = 512 * (i + 1)
                sol[pl.ds(512 * i, 512), cols] = jnp.dot(
                    pan[D0, pl.ds(512 * i, 512), :deep], pan[R0, :deep, cols],
                    preferred_element_type=F32,
                ).astype(BF)

    def carried():
        @pl.loop(0, 4)
        def _(n):
            cols = pl.ds(pl.multiple_of(n * 256, 256), 256)
            for i in (0, 1):
                rows = pl.ds(512 * i, 512)
                car[rows, cols] = (
                    pan[R1, rows, cols].astype(F32)
                    - jnp.dot(pan[CP, rows, :], sol[:1024, cols], preferred_element_type=F32)
                ).astype(BF)

    def second():
        @pl.loop(0, 4)
        def _(n):
            cols = pl.ds(pl.multiple_of(n * 256, 256), 256)
            for i in (0, 1):
                deep = 512 * (i + 1)
                sol[pl.ds(1024 + 512 * i, 512), cols] = jnp.dot(
                    pan[D1, pl.ds(512 * i, 512), :deep], car[:deep, cols],
                    preferred_element_type=F32,
                ).astype(BF)

    def product(half, rows, cols):
        left = jnp.concatenate([fac[8 * half + b, rows, :] for b in range(8)], axis=1)
        return jnp.dot(left, sol[pl.ds(1024 * half, 1024), cols], preferred_element_type=F32)

    def update_first():
        @pl.loop(0, 4)
        def _(n):
            cols = pl.ds(pl.multiple_of(n * 256, 256), 256)
            for i in (0, 1):
                rows = pl.ds(512 * i, 512)
                acc[rows, cols] = trail[rows, cols].astype(F32) - product(0, rows, cols)

    def stored(n):
        cols = pl.ds(pl.multiple_of(n * 256, 256), 256)
        return pltpu.make_async_copy(out.at[:, cols], upd_ref.at[:, cols], local.at[9 + n])

    def update_second():
        @pl.loop(0, 4)
        def _(n):
            cols = pl.ds(pl.multiple_of(n * 256, 256), 256)
            for i in (0, 1):
                rows = pl.ds(512 * i, 512)
                out[rows, cols] = (acc[rows, cols] - product(1, rows, cols)).astype(BF)
            stored(n).start()

    loads[0].wait()
    loads[1].wait()
    own(0)
    loads[2].wait()
    lown()
    pair(0)
    line(0)
    hop(0, 1)
    loads[3].wait()
    loads[4].wait()
    loads[5].wait()
    own(1)
    line(1)
    hop(0, 2)
    line(2)
    pair(1)
    hop(0, 3)
    ring(0)
    hop(0, 4)
    hop(1, 1)
    own(2)
    fill(0)
    first()
    keep = [pltpu.make_async_copy(sol.at[mine, :], solved_ref.at[0], local.at[7])]
    keep[0].start()
    hop(1, 2)
    ring(1)
    pair(2)
    hop(1, 3)
    ring(2)
    hop(1, 4)
    hop(2, 1)
    fill(1)
    carried()
    hop(2, 2)
    ring(3)
    ringlast()
    hop(2, 3)
    loads[6].wait()
    update_first()
    hop(2, 4)
    fill(2)
    second()
    low = pl.ds(pl.multiple_of(1024 + row * 32, 32), 32)
    keep.append(pltpu.make_async_copy(sol.at[low, :], solved_ref.at[1], local.at[8]))
    keep[1].start()
    update_second()
    for copy in sent:
        copy.wait_send()

    @pl.when(mid)
    def _():
        for c, to, at in later:
            lcopy(c, to, lsend.at[at]).wait_send()

    for copy in keep:
        copy.wait()
    for n in range(4):
        stored(n).wait()


def shards(rhs_top, diag_inverse, panel_coupling, trailing_factor, rhs_trailing):
    anywhere = pl.BlockSpec(memory_space=pl.ANY)
    dma = pltpu.SemaphoreType.DMA
    return pl.pallas_call(
        kernel,
        out_shape=(
            jax.ShapeDtypeStruct((2, 32, 1024), BF),
            jax.ShapeDtypeStruct((1024, 1024), BF),
        ),
        in_specs=[anywhere] * 5,
        out_specs=(anywhere, anywhere),
        scratch_shapes=[
            pltpu.VMEM((5, 1024, 1024), BF),
            pltpu.VMEM((2048, 1024), BF),
            pltpu.VMEM((1024, 1024), BF),
            pltpu.VMEM((16, 1024, 128), BF),
            pltpu.VMEM((1024, 1024), BF),
            pltpu.VMEM((1024, 1024), F32),
            pltpu.VMEM((1024, 1024), BF),
            dma((3, 32)),
            dma((16,)),
            dma((93,)),
            dma((17,)),
            dma((13,)),
        ],
        compiler_params=pltpu.CompilerParams(
            collective_id=0, has_side_effects=True, vmem_limit_bytes=50 * 1024 * 1024
        ),
        name="substitute",
    )(rhs_top, diag_inverse, panel_coupling, trailing_factor, rhs_trailing)


def solution(mesh):
    in_specs = (
        P(None, "row", "col"),
        P(None, "row", None),
        P("row", None),
        P("row", "col"),
        P("row", "col"),
    )
    out_specs = (P(None, "row", "col"), P("row", "col"))
    return jax.shard_map(shards, mesh=mesh, in_specs=in_specs, out_specs=out_specs, check_vma=False)
```

```python
import jax
import jax.numpy as jnp
from jax import lax
from jax.experimental import pallas as pl
from jax.experimental.pallas import tpu as pltpu
from jax.sharding import PartitionSpec as P

MESH = pl.DeviceIdType.MESH
BF = jnp.bfloat16
F32 = jnp.float32

RHS0, INV0, MID, INV1 = range(4)
STAGES = ((RHS0, INV0), (MID,), (INV1,))


def kernel(
    rhs_ref, diag_ref, coup_ref, fac_ref, trail_ref,
    solved_ref, upd_ref,
    pan, dia, sol, car, fac, trail, acc, out,
    recv, lrecv, send, lsend, local, kept, stores,
):
    row = lax.axis_index("row")
    col = lax.axis_index("col")
    z, yh, k = row // 4, (row // 2) % 2, row % 2
    x, yl = col // 4, col % 4
    mid = (yl // 2 + yl % 2) % 2 == 1
    sib = row + 1 - 2 * k
    zup, zdn = (row + 4) % 32, (row + 28) % 32
    mate = row + 2 - 4 * yh
    xup, xdn = (col + 4) % 16, (col + 12) % 16
    y1 = x * 4 + yl + 1 - 2 * (yl % 2)
    y2 = x * 4 + 3 - yl

    def rows_of(q):
        return pl.ds(pl.multiple_of(q * 32, 32), 32)

    mine = rows_of(row)

    def inverse_loads(p, at):
        return [
            pltpu.make_async_copy(
                diag_ref.at[p, :, pl.ds(256 * j, 256)], dia.at[p, j, mine, :], local.at[at + j]
            )
            for j in range(4)
        ]

    load_a = [pltpu.make_async_copy(rhs_ref.at[0], pan.at[0, mine, :], local.at[0])] + inverse_loads(0, 1)
    load_f = [pltpu.make_async_copy(fac_ref, fac.at[col], local.at[5])]
    load_b = [
        pltpu.make_async_copy(coup_ref, pan.at[1, mine, :], local.at[6]),
        pltpu.make_async_copy(rhs_ref.at[1], pan.at[2, mine, :], local.at[7]),
    ]
    load_c = inverse_loads(1, 8)
    load_t = [pltpu.make_async_copy(trail_ref, trail, local.at[12])]
    for load in load_a + load_f + load_b + load_c + load_t:
        load.start()

    def ready(loads):
        for load in loads:
            load.wait()

    barrier = pltpu.get_barrier_semaphore()
    peers = [(sib, col), (zup, col), (zdn, col), (mate, col), (row, xup), (row, xdn), (row, y1)]
    for peer in peers:
        pl.semaphore_signal(barrier, inc=1, device_id=peer, device_id_type=MESH)

    @pl.when(mid)
    def _():
        pl.semaphore_signal(barrier, inc=1, device_id=(row, y2), device_id_type=MESH)
        pl.semaphore_wait(barrier, len(peers) + 1)

    @pl.when(jnp.logical_not(mid))
    def _():
        pl.semaphore_wait(barrier, len(peers))

    def view(flow, q, chunks):
        if flow == RHS0:
            return pan.at[0, rows_of(q), :]
        if flow == MID:
            return pan.at[1:3, rows_of(q), :]
        return dia.at[0 if flow == INV0 else 1, 0:chunks, rows_of(q), :]

    def each_size(flow, q, act):
        if flow in (RHS0, MID):
            act(0)
        else:
            for chunks in (1, 2, 3, 4):

                @pl.when(q // 8 + 1 == chunks)
                def _(chunks=chunks):
                    act(chunks)

    def pcopy(flow, q, to, at, chunks):
        return pltpu.make_async_remote_copy(
            src_ref=view(flow, q, chunks), dst_ref=view(flow, q, chunks),
            send_sem=send.at[at], recv_sem=recv.at[flow, q],
            device_id=(to, col), device_id_type=MESH,
        )

    sent = []
    used = [0]

    def push(flow, q, targets):
        first_at = used[0]
        used[0] += len(targets)

        def act(chunks):
            for i, to in enumerate(targets):
                pcopy(flow, q, to, first_at + i, chunks).start()

        each_size(flow, q, act)
        sent.append((flow, q, targets, first_at))

    def arrive(flow, q):
        each_size(flow, q, lambda chunks: pcopy(flow, q, sib, 0, chunks).wait_recv())

    def own(stage):
        for flow in STAGES[stage]:
            push(flow, row, (zup, zdn, mate, sib))

    def pair(stage):
        for flow in STAGES[stage]:
            arrive(flow, mate)
            push(flow, mate, (zup, zdn, sib))

    def hop(stage, h, j):
        lane = (yh + j * (1 - 2 * yh)) * 2 + k
        for flow in STAGES[stage]:
            if h < 4 or j == 0:
                q = (z + 8 - h) % 8 * 4 + lane
                arrive(flow, q)
                push(flow, q, (zup, sib) if h < 3 or (h == 3 and j == 0) else (sib,))
            if h < 4 or j == 1:
                q = (z + h) % 8 * 4 + lane
                arrive(flow, q)
                push(flow, q, (zdn, sib) if h < 3 or (h == 3 and j == 1) else (sib,))

    def fill(stage):
        @pl.loop(0, 16)
        def _(i):
            for flow in STAGES[stage]:
                arrive(flow, i * 2 + 1 - k)

    def lcopy(c, to, at):
        return pltpu.make_async_remote_copy(
            src_ref=fac.at[c], dst_ref=fac.at[c],
            send_sem=lsend.at[at], recv_sem=lrecv.at[c],
            device_id=(row, to), device_id_type=MESH,
        )

    always, middle = [], []

    def lpush(c, to, record):
        at = len(always) + len(middle)
        lcopy(c, to, at).start()
        record.append((c, to, at))

    def larrive(c):
        lcopy(c, xup, 0).wait_recv()

    def spread(c, inner):
        @pl.when(mid)
        def _():
            lpush(c, inner, middle)

        lpush(c, xup, always)
        lpush(c, xdn, always)

    def lown():
        lpush(col, y1, always)
        spread(col, y2)

    order = [yl, yl + 1 - 2 * (yl % 2), 2 - yl // 2, 3 - 3 * (yl // 2)]

    def line(d):
        c = x * 4 + order[d]
        larrive(c)
        spread(c, y2 if d == 1 else y1)

    def ring(m):
        below = (x + 3) % 4 * 4 + order[m]
        above = (x + 1) % 4 * 4 + order[m]
        larrive(below)
        if m % 2 == 0:
            lpush(below, xup, always)
        larrive(above)
        if m % 2 == 1:
            lpush(above, xdn, always)

    def ringlast():
        for e in order:
            larrive((x + 2) % 4 * 4 + e)

    def lower(p, i, right):
        left = jnp.concatenate([dia[p, j, pl.ds(256 * i, 256), :] for j in range(i + 1)], axis=1)
        return jnp.dot(left, right, preferred_element_type=F32).astype(BF)

    def first(i):
        sol[pl.ds(256 * i, 256), :] = lower(0, i, pan[0, : 256 * (i + 1), :])

    def second(i):
        sol[pl.ds(1024 + 256 * i, 256), :] = lower(1, i, car[: 256 * (i + 1), :])

    def carried(low, high):
        @pl.loop(low, high)
        def _(i):
            rows = pl.ds(pl.multiple_of(i * 256, 256), 256)
            car[rows, :] = (
                pan[2, rows, :].astype(F32)
                - jnp.dot(pan[1, rows, :], sol[:1024, :], preferred_element_type=F32)
            ).astype(BF)

    def product(half, rows):
        left = jnp.concatenate([fac[8 * half + b, rows, :] for b in range(8)], axis=1)
        return jnp.dot(left, sol[pl.ds(1024 * half, 1024), :], preferred_element_type=F32)

    def update_first(low, high):
        @pl.loop(low, high)
        def _(i):
            rows = pl.ds(pl.multiple_of(i * 256, 256), 256)
            acc[rows, :] = trail[rows, :].astype(F32) - product(0, rows)

    def stored(i):
        rows = pl.ds(pl.multiple_of(i * 256, 256), 256)
        return pltpu.make_async_copy(out.at[rows, :], upd_ref.at[rows, :], stores.at[i])

    def update_second():
        @pl.loop(0, 4)
        def _(i):
            rows = pl.ds(pl.multiple_of(i * 256, 256), 256)
            out[rows, :] = (acc[rows, :] - product(1, rows)).astype(BF)
            stored(i).start()

    def keep(p):
        rows = pl.ds(pl.multiple_of(1024 * p + row * 32, 32), 32)
        return pltpu.make_async_copy(sol.at[rows, :], solved_ref.at[p], kept.at[p])

    ready(load_a)
    own(0)
    ready(load_f)
    lown()
    ready(load_b)
    own(1)
    ready(load_c)
    hop(0, 1, 0)
    pair(0)
    line(1)
    hop(0, 2, 0)
    ring(0)
    hop(0, 1, 1)
    hop(0, 3, 0)
    line(2)
    hop(0, 2, 1)
    hop(0, 4, 0)
    ring(1)
    pair(1)
    hop(1, 1, 0)
    own(2)
    hop(0, 3, 1)
    line(3)
    hop(1, 2, 0)
    hop(0, 4, 1)
    ring(2)
    hop(1, 1, 1)
    fill(0)
    first(0)
    first(1)
    hop(1, 3, 0)
    first(2)
    hop(1, 2, 1)
    first(3)
    keep(0).start()
    pair(2)
    hop(1, 4, 0)
    hop(2, 1, 0)
    ring(3)
    hop(1, 3, 1)
    hop(2, 2, 0)
    hop(1, 4, 1)
    hop(2, 1, 1)
    fill(1)
    carried(0, 2)
    hop(2, 3, 0)
    carried(2, 4)
    hop(2, 2, 1)
    hop(2, 4, 0)
    ringlast()
    ready(load_t)
    update_first(0, 2)
    hop(2, 3, 1)
    update_first(2, 4)
    hop(2, 4, 1)
    fill(2)
    for i in range(4):
        second(i)
    keep(1).start()
    update_second()

    for flow, q, targets, first_at in sent:

        def act(chunks, flow=flow, q=q, targets=targets, first_at=first_at):
            for i, to in enumerate(targets):
                pcopy(flow, q, to, first_at + i, chunks).wait_send()

        each_size(flow, q, act)
    for c, to, at in always:
        lcopy(c, to, at).wait_send()

    @pl.when(mid)
    def _():
        for c, to, at in middle:
            lcopy(c, to, at).wait_send()

    keep(0).wait()
    keep(1).wait()
    for i in range(4):
        stored(i).wait()


def shards(rhs_top, diag_inverse, panel_coupling, trailing_factor, rhs_trailing):
    anywhere = pl.BlockSpec(memory_space=pl.ANY)
    dma = pltpu.SemaphoreType.DMA
    return pl.pallas_call(
        kernel,
        out_shape=(
            jax.ShapeDtypeStruct((2, 32, 1024), BF),
            jax.ShapeDtypeStruct((1024, 1024), BF),
        ),
        in_specs=[anywhere] * 5,
        out_specs=(anywhere, anywhere),
        scratch_shapes=[
            pltpu.VMEM((3, 1024, 1024), BF),
            pltpu.VMEM((2, 4, 1024, 256), BF),
            pltpu.VMEM((2048, 1024), BF),
            pltpu.VMEM((1024, 1024), BF),
            pltpu.VMEM((16, 1024, 128), BF),
            pltpu.VMEM((1024, 1024), BF),
            pltpu.VMEM((1024, 1024), F32),
            pltpu.VMEM((1024, 1024), BF),
            dma((4, 32)),
            dma((16,)),
            dma((124,)),
            dma((17,)),
            dma((13,)),
            dma((2,)),
            dma((4,)),
        ],
        compiler_params=pltpu.CompilerParams(
            collective_id=0, has_side_effects=True, vmem_limit_bytes=60 * 1024 * 1024
        ),
        name="substitute",
    )(rhs_top, diag_inverse, panel_coupling, trailing_factor, rhs_trailing)


def solution(mesh):
    in_specs = (
        P(None, "row", "col"),
        P(None, "row", None),
        P("row", None),
        P("row", "col"),
        P("row", "col"),
    )
    out_specs = (P(None, "row", "col"), P("row", "col"))
    return jax.shard_map(shards, mesh=mesh, in_specs=in_specs, out_specs=out_specs, check_vma=False)
```

```python
import jax
import jax.numpy as jnp
from jax import lax
from jax.experimental import pallas as pl
from jax.experimental.pallas import tpu as pltpu
from jax.sharding import PartitionSpec as P

MESH = pl.DeviceIdType.MESH
BF = jnp.bfloat16
F32 = jnp.float32

RHS0, INV0, MID, INV1 = range(4)
STAGES = ((RHS0, INV0), (MID,), (INV1,))


def kernel(
    rhs_ref, diag_ref, coup_ref, fac_ref, trail_ref,
    solved_ref, upd_ref,
    pan, dia, sol, car, fac, trail, acc, out,
    recv, lrecv, send, lsend, local, kept, stores,
):
    row = lax.axis_index("row")
    col = lax.axis_index("col")
    z, yh, k = row // 4, (row // 2) % 2, row % 2
    x, yl = col // 4, col % 4
    mid = (yl // 2 + yl % 2) % 2 == 1
    sib = row + 1 - 2 * k
    zup, zdn = (row + 4) % 32, (row + 28) % 32
    mate = row + 2 - 4 * yh
    xup, xdn = (col + 4) % 16, (col + 12) % 16
    y1 = x * 4 + yl + 1 - 2 * (yl % 2)
    y2 = x * 4 + 3 - yl

    def rows_of(q):
        return pl.ds(pl.multiple_of(q * 32, 32), 32)

    mine = rows_of(row)

    def inverse_loads(p, at):
        return [
            pltpu.make_async_copy(
                diag_ref.at[p, :, pl.ds(256 * j, 256)], dia.at[p, j, mine, :], local.at[at + j]
            )
            for j in range(4)
        ]

    load_a = [pltpu.make_async_copy(rhs_ref.at[0], pan.at[0, mine, :], local.at[0])] + inverse_loads(0, 1)
    load_f = [pltpu.make_async_copy(fac_ref, fac.at[col], local.at[5])]
    load_b = [
        pltpu.make_async_copy(coup_ref, pan.at[1, mine, :], local.at[6]),
        pltpu.make_async_copy(rhs_ref.at[1], pan.at[2, mine, :], local.at[7]),
    ]
    load_c = inverse_loads(1, 8)
    load_t = [pltpu.make_async_copy(trail_ref, trail, local.at[12])]
    for load in load_a + load_f + load_b + load_c + load_t:
        load.start()

    def ready(loads):
        for load in loads:
            load.wait()

    barrier = pltpu.get_barrier_semaphore()
    peers = [(sib, col), (zup, col), (zdn, col), (mate, col), (row, xup), (row, xdn), (row, y1)]
    for peer in peers:
        pl.semaphore_signal(barrier, inc=1, device_id=peer, device_id_type=MESH)

    @pl.when(mid)
    def _():
        pl.semaphore_signal(barrier, inc=1, device_id=(row, y2), device_id_type=MESH)
        pl.semaphore_wait(barrier, len(peers) + 1)

    @pl.when(jnp.logical_not(mid))
    def _():
        pl.semaphore_wait(barrier, len(peers))

    def view(flow, q, chunks):
        if flow == RHS0:
            return pan.at[0, rows_of(q), :]
        if flow == MID:
            return pan.at[1:3, rows_of(q), :]
        return dia.at[0 if flow == INV0 else 1, 0:chunks, rows_of(q), :]

    def each_size(flow, q, act):
        if flow in (RHS0, MID):
            act(0)
        else:
            for chunks in (1, 2, 3, 4):

                @pl.when(q // 8 + 1 == chunks)
                def _(chunks=chunks):
                    act(chunks)

    def pcopy(flow, q, to, at, chunks):
        return pltpu.make_async_remote_copy(
            src_ref=view(flow, q, chunks), dst_ref=view(flow, q, chunks),
            send_sem=send.at[at], recv_sem=recv.at[flow, q],
            device_id=(to, col), device_id_type=MESH,
        )

    sent = []
    used = [0]

    def push(flow, q, targets):
        first_at = used[0]
        used[0] += len(targets)

        def act(chunks):
            for i, to in enumerate(targets):
                pcopy(flow, q, to, first_at + i, chunks).start()

        each_size(flow, q, act)
        sent.append((flow, q, targets, first_at))

    def arrive(flow, q):
        each_size(flow, q, lambda chunks: pcopy(flow, q, sib, 0, chunks).wait_recv())

    def own(stage):
        for flow in STAGES[stage]:
            push(flow, row, (zup, zdn, mate, sib))

    def pair(stage):
        for flow in STAGES[stage]:
            arrive(flow, mate)
            push(flow, mate, (zup, zdn, sib))

    def hop(stage, h, j):
        lane = (yh + j * (1 - 2 * yh)) * 2 + k
        for flow in STAGES[stage]:
            if h < 4 or j == 0:
                q = (z + 8 - h) % 8 * 4 + lane
                arrive(flow, q)
                push(flow, q, (zup, sib) if h < 3 or (h == 3 and j == 0) else (sib,))
            if h < 4 or j == 1:
                q = (z + h) % 8 * 4 + lane
                arrive(flow, q)
                push(flow, q, (zdn, sib) if h < 3 or (h == 3 and j == 1) else (sib,))

    def fill(stage):
        @pl.loop(0, 16)
        def _(i):
            for flow in STAGES[stage]:
                arrive(flow, i * 2 + 1 - k)

    def lcopy(c, to, at):
        return pltpu.make_async_remote_copy(
            src_ref=fac.at[c], dst_ref=fac.at[c],
            send_sem=lsend.at[at], recv_sem=lrecv.at[c],
            device_id=(row, to), device_id_type=MESH,
        )

    always, middle = [], []

    def lpush(c, to, record):
        at = len(always) + len(middle)
        lcopy(c, to, at).start()
        record.append((c, to, at))

    def larrive(c):
        lcopy(c, xup, 0).wait_recv()

    def spread(c, inner):
        @pl.when(mid)
        def _():
            lpush(c, inner, middle)

        lpush(c, xup, always)
        lpush(c, xdn, always)

    def lown():
        lpush(col, y1, always)
        spread(col, y2)

    order = [yl, yl + 1 - 2 * (yl % 2), 2 - yl // 2, 3 - 3 * (yl // 2)]

    def line(d):
        c = x * 4 + order[d]
        larrive(c)
        spread(c, y2 if d == 1 else y1)

    def ring(m):
        below = (x + 3) % 4 * 4 + order[m]
        above = (x + 1) % 4 * 4 + order[m]
        larrive(below)
        if m % 2 == 0:
            lpush(below, xup, always)
        larrive(above)
        if m % 2 == 1:
            lpush(above, xdn, always)

    def ringlast():
        for e in order:
            larrive((x + 2) % 4 * 4 + e)

    def lower(p, i, right):
        left = jnp.concatenate([dia[p, j, pl.ds(256 * i, 256), :] for j in range(i + 1)], axis=1)
        return jnp.dot(left, right, preferred_element_type=F32).astype(BF)

    def first(i):
        sol[pl.ds(256 * i, 256), :] = lower(0, i, pan[0, : 256 * (i + 1), :])

    def second(i):
        sol[pl.ds(1024 + 256 * i, 256), :] = lower(1, i, car[: 256 * (i + 1), :])

    def carried(low, high):
        @pl.loop(low, high)
        def _(i):
            rows = pl.ds(pl.multiple_of(i * 256, 256), 256)
            car[rows, :] = (
                pan[2, rows, :].astype(F32)
                - jnp.dot(pan[1, rows, :], sol[:1024, :], preferred_element_type=F32)
            ).astype(BF)

    def product(half, rows):
        left = jnp.concatenate([fac[8 * half + b, rows, :] for b in range(8)], axis=1)
        return jnp.dot(left, sol[pl.ds(1024 * half, 1024), :], preferred_element_type=F32)

    def update_first(low, high):
        @pl.loop(low, high)
        def _(i):
            rows = pl.ds(pl.multiple_of(i * 256, 256), 256)
            acc[rows, :] = trail[rows, :].astype(F32) - product(0, rows)

    def stored(i):
        rows = pl.ds(pl.multiple_of(i * 256, 256), 256)
        return pltpu.make_async_copy(out.at[rows, :], upd_ref.at[rows, :], stores.at[i])

    def update_second():
        @pl.loop(0, 4)
        def _(i):
            rows = pl.ds(pl.multiple_of(i * 256, 256), 256)
            out[rows, :] = (acc[rows, :] - product(1, rows)).astype(BF)
            stored(i).start()

    def keep(p):
        rows = pl.ds(pl.multiple_of(1024 * p + row * 32, 32), 32)
        return pltpu.make_async_copy(sol.at[rows, :], solved_ref.at[p], kept.at[p])

    ready(load_a)
    own(0)
    ready(load_f)
    lown()
    ready(load_b)
    own(1)
    ready(load_c)
    hop(0, 1, 0)
    pair(0)
    hop(0, 2, 0)
    hop(1, 1, 0)
    line(1)
    ring(0)
    own(2)
    hop(0, 1, 1)
    pair(1)
    hop(0, 3, 0)
    hop(1, 2, 0)
    hop(2, 1, 0)
    line(2)
    ring(1)
    hop(0, 2, 1)
    hop(1, 1, 1)
    pair(2)
    hop(0, 4, 0)
    hop(1, 3, 0)
    hop(2, 2, 0)
    line(3)
    ring(2)
    hop(0, 3, 1)
    hop(1, 2, 1)
    hop(2, 1, 1)
    hop(1, 4, 0)
    hop(2, 3, 0)
    ring(3)
    hop(0, 4, 1)
    hop(1, 3, 1)
    hop(2, 2, 1)
    hop(2, 4, 0)
    fill(0)
    first(0)
    first(1)
    first(2)
    first(3)
    keep(0).start()
    hop(1, 4, 1)
    hop(2, 3, 1)
    fill(1)
    carried(0, 4)
    ringlast()
    ready(load_t)
    update_first(0, 2)
    hop(2, 4, 1)
    update_first(2, 4)
    fill(2)
    second(0)
    second(1)
    second(2)
    second(3)
    keep(1).start()
    update_second()

    for flow, q, targets, first_at in sent:

        def act(chunks, flow=flow, q=q, targets=targets, first_at=first_at):
            for i, to in enumerate(targets):
                pcopy(flow, q, to, first_at + i, chunks).wait_send()

        each_size(flow, q, act)
    for c, to, at in always:
        lcopy(c, to, at).wait_send()

    @pl.when(mid)
    def _():
        for c, to, at in middle:
            lcopy(c, to, at).wait_send()

    keep(0).wait()
    keep(1).wait()
    for i in range(4):
        stored(i).wait()


def shards(rhs_top, diag_inverse, panel_coupling, trailing_factor, rhs_trailing):
    anywhere = pl.BlockSpec(memory_space=pl.ANY)
    dma = pltpu.SemaphoreType.DMA
    return pl.pallas_call(
        kernel,
        out_shape=(
            jax.ShapeDtypeStruct((2, 32, 1024), BF),
            jax.ShapeDtypeStruct((1024, 1024), BF),
        ),
        in_specs=[pl.BlockSpec(memory_space=pltpu.HBM)] * 5,
        out_specs=(anywhere, anywhere),
        scratch_shapes=[
            pltpu.VMEM((3, 1024, 1024), BF),
            pltpu.VMEM((2, 4, 1024, 256), BF),
            pltpu.VMEM((2048, 1024), BF),
            pltpu.VMEM((1024, 1024), BF),
            pltpu.VMEM((16, 1024, 128), BF),
            pltpu.VMEM((1024, 1024), BF),
            pltpu.VMEM((1024, 1024), F32),
            pltpu.VMEM((1024, 1024), BF),
            dma((4, 32)),
            dma((16,)),
            dma((124,)),
            dma((17,)),
            dma((13,)),
            dma((2,)),
            dma((4,)),
        ],
        compiler_params=pltpu.CompilerParams(
            collective_id=0, has_side_effects=True, vmem_limit_bytes=50 * 1024 * 1024
        ),
        name="substitute",
    )(rhs_top, diag_inverse, panel_coupling, trailing_factor, rhs_trailing)


def solution(mesh):
    in_specs = (
        P(None, "row", "col"),
        P(None, "row", None),
        P("row", None),
        P("row", "col"),
        P("row", "col"),
    )
    out_specs = (P(None, "row", "col"), P("row", "col"))
    return jax.shard_map(shards, mesh=mesh, in_specs=in_specs, out_specs=out_specs, check_vma=False)
```

```python
import jax
import jax.numpy as jnp
from jax import lax
from jax.experimental import pallas as pl
from jax.experimental.pallas import tpu as pltpu
from jax.sharding import PartitionSpec as P

MESH = pl.DeviceIdType.MESH
BF = jnp.bfloat16
F32 = jnp.float32

RHS0, INV0, MID, INV1 = range(4)
STAGES = ((RHS0, INV0), (MID,), (INV1,))


def kernel(
    rhs_ref, diag_ref, coup_ref, fac_ref, trail_ref,
    solved_ref, upd_ref,
    pan, dia, sol, car, fac, trail, acc, out,
    recv, lrecv, send, lsend, local, kept, stores,
):
    row = lax.axis_index("row")
    col = lax.axis_index("col")
    z, yh, k = row // 4, (row // 2) % 2, row % 2
    x, yl = col // 4, col % 4
    mid = (yl // 2 + yl % 2) % 2 == 1
    sib = row + 1 - 2 * k
    zup, zdn = (row + 4) % 32, (row + 28) % 32
    mate = row + 2 - 4 * yh
    xup, xdn = (col + 4) % 16, (col + 12) % 16
    y1 = x * 4 + yl + 1 - 2 * (yl % 2)
    y2 = x * 4 + 3 - yl

    def rows_of(q):
        return pl.ds(pl.multiple_of(q * 32, 32), 32)

    mine = rows_of(row)

    def inverse_loads(p, at):
        return [
            pltpu.make_async_copy(
                diag_ref.at[p, :, pl.ds(256 * j, 256)], dia.at[p, j, mine, :], local.at[at + j]
            )
            for j in range(4)
        ]

    load_a = [pltpu.make_async_copy(rhs_ref.at[0], pan.at[0, mine, :], local.at[0])] + inverse_loads(0, 1)
    load_f = [pltpu.make_async_copy(fac_ref, fac.at[col], local.at[5])]
    load_b = [
        pltpu.make_async_copy(coup_ref, pan.at[1, mine, :], local.at[6]),
        pltpu.make_async_copy(rhs_ref.at[1], pan.at[2, mine, :], local.at[7]),
    ]
    load_c = inverse_loads(1, 8)
    load_t = [pltpu.make_async_copy(trail_ref, trail, local.at[12])]
    for load in load_a + load_f + load_b + load_c + load_t:
        load.start()

    def ready(loads):
        for load in loads:
            load.wait()

    barrier = pltpu.get_barrier_semaphore()
    peers = [(sib, col), (zup, col), (zdn, col), (mate, col), (row, xup), (row, xdn), (row, y1)]
    for peer in peers:
        pl.semaphore_signal(barrier, inc=1, device_id=peer, device_id_type=MESH)

    @pl.when(mid)
    def _():
        pl.semaphore_signal(barrier, inc=1, device_id=(row, y2), device_id_type=MESH)
        pl.semaphore_wait(barrier, len(peers) + 1)

    @pl.when(jnp.logical_not(mid))
    def _():
        pl.semaphore_wait(barrier, len(peers))

    def view(flow, q, chunks):
        if flow == RHS0:
            return pan.at[0, rows_of(q), :]
        if flow == MID:
            return pan.at[1:3, rows_of(q), :]
        return dia.at[0 if flow == INV0 else 1, 0:chunks, rows_of(q), :]

    def each_size(flow, q, act):
        if flow in (RHS0, MID):
            act(0)
        else:
            for chunks in (1, 2, 3, 4):

                @pl.when(q // 8 + 1 == chunks)
                def _(chunks=chunks):
                    act(chunks)

    def pcopy(flow, q, to, at, chunks):
        return pltpu.make_async_remote_copy(
            src_ref=view(flow, q, chunks), dst_ref=view(flow, q, chunks),
            send_sem=send.at[at], recv_sem=recv.at[flow, q],
            device_id=(to, col), device_id_type=MESH,
        )

    sent = []
    used = [0]

    def push(flow, q, targets):
        first_at = used[0]
        used[0] += len(targets)

        def act(chunks):
            for i, to in enumerate(targets):
                pcopy(flow, q, to, first_at + i, chunks).start()

        each_size(flow, q, act)
        sent.append((flow, q, targets, first_at))

    def arrive(flow, q):
        each_size(flow, q, lambda chunks: pcopy(flow, q, sib, 0, chunks).wait_recv())

    def own(stage):
        for flow in STAGES[stage]:
            push(flow, row, (zup, zdn, mate, sib))

    def pair(stage):
        for flow in STAGES[stage]:
            arrive(flow, mate)
            push(flow, mate, (zup, zdn, sib))

    def hop(stage, h, j):
        lane = (yh + j * (1 - 2 * yh)) * 2 + k
        for flow in STAGES[stage]:
            if h < 4 or j == 0:
                q = (z + 8 - h) % 8 * 4 + lane
                arrive(flow, q)
                push(flow, q, (zup, sib) if h < 3 or (h == 3 and j == 0) else (sib,))
            if h < 4 or j == 1:
                q = (z + h) % 8 * 4 + lane
                arrive(flow, q)
                push(flow, q, (zdn, sib) if h < 3 or (h == 3 and j == 1) else (sib,))

    def fill(stage):
        @pl.loop(0, 16)
        def _(i):
            for flow in STAGES[stage]:
                arrive(flow, i * 2 + 1 - k)

    def lcopy(c, to, at):
        return pltpu.make_async_remote_copy(
            src_ref=fac.at[c], dst_ref=fac.at[c],
            send_sem=lsend.at[at], recv_sem=lrecv.at[c],
            device_id=(row, to), device_id_type=MESH,
        )

    always, middle = [], []

    def lpush(c, to, record):
        at = len(always) + len(middle)
        lcopy(c, to, at).start()
        record.append((c, to, at))

    def larrive(c):
        lcopy(c, xup, 0).wait_recv()

    def spread(c, inner):
        @pl.when(mid)
        def _():
            lpush(c, inner, middle)

        lpush(c, xup, always)
        lpush(c, xdn, always)

    def lown():
        lpush(col, y1, always)
        spread(col, y2)

    order = [yl, yl + 1 - 2 * (yl % 2), 2 - yl // 2, 3 - 3 * (yl // 2)]

    def line(d):
        c = x * 4 + order[d]
        larrive(c)
        spread(c, y2 if d == 1 else y1)

    def ring(m):
        below = (x + 3) % 4 * 4 + order[m]
        above = (x + 1) % 4 * 4 + order[m]
        larrive(below)
        if m % 2 == 0:
            lpush(below, xup, always)
        larrive(above)
        if m % 2 == 1:
            lpush(above, xdn, always)

    def ringlast():
        for e in order:
            larrive((x + 2) % 4 * 4 + e)

    def lower(p, i, right):
        left = jnp.concatenate([dia[p, j, pl.ds(256 * i, 256), :] for j in range(i + 1)], axis=1)
        return jnp.dot(left, right, preferred_element_type=F32).astype(BF)

    def first(i):
        sol[pl.ds(256 * i, 256), :] = lower(0, i, pan[0, : 256 * (i + 1), :])

    def second(i):
        sol[pl.ds(1024 + 256 * i, 256), :] = lower(1, i, car[: 256 * (i + 1), :])

    def carried(low, high):
        @pl.loop(low, high)
        def _(i):
            rows = pl.ds(pl.multiple_of(i * 256, 256), 256)
            car[rows, :] = (
                pan[2, rows, :].astype(F32)
                - jnp.dot(pan[1, rows, :], sol[:1024, :], preferred_element_type=F32)
            ).astype(BF)

    def product(half, rows):
        left = jnp.concatenate([fac[8 * half + b, rows, :] for b in range(8)], axis=1)
        return jnp.dot(left, sol[pl.ds(1024 * half, 1024), :], preferred_element_type=F32)

    def update_first(low, high):
        @pl.loop(low, high)
        def _(i):
            rows = pl.ds(pl.multiple_of(i * 256, 256), 256)
            acc[rows, :] = trail[rows, :].astype(F32) - product(0, rows)

    def stored(i):
        rows = pl.ds(pl.multiple_of(i * 256, 256), 256)
        return pltpu.make_async_copy(out.at[rows, :], upd_ref.at[rows, :], stores.at[i])

    def update_second():
        @pl.loop(0, 4)
        def _(i):
            rows = pl.ds(pl.multiple_of(i * 256, 256), 256)
            out[rows, :] = (acc[rows, :] - product(1, rows)).astype(BF)
            stored(i).start()

    def keep(p):
        rows = pl.ds(pl.multiple_of(1024 * p + row * 32, 32), 32)
        return pltpu.make_async_copy(sol.at[rows, :], solved_ref.at[p], kept.at[p])

    ready(load_a)
    own(0)
    ready(load_f)
    lown()
    ready(load_b)
    own(1)
    ready(load_c)
    hop(0, 1, 0)
    pair(0)
    hop(0, 2, 0)
    hop(1, 1, 0)
    line(1)
    ring(0)
    own(2)
    hop(0, 1, 1)
    pair(1)
    hop(0, 3, 0)
    hop(1, 2, 0)
    hop(2, 1, 0)
    line(2)
    ring(1)
    hop(0, 2, 1)
    hop(1, 1, 1)
    pair(2)
    hop(0, 4, 0)
    hop(1, 3, 0)
    hop(2, 2, 0)
    line(3)
    ring(2)
    hop(0, 3, 1)
    hop(1, 2, 1)
    hop(2, 1, 1)
    hop(1, 4, 0)
    hop(2, 3, 0)
    ring(3)
    hop(0, 4, 1)
    hop(1, 3, 1)
    hop(2, 2, 1)
    hop(2, 4, 0)
    fill(0)
    first(0)
    first(1)
    first(2)
    first(3)
    keep(0).start()
    hop(2, 3, 1)
    ringlast()
    ready(load_t)
    update_first(0, 2)
    hop(1, 4, 1)
    fill(1)
    carried(0, 4)
    hop(2, 4, 1)
    update_first(2, 4)
    fill(2)
    second(0)
    second(1)
    second(2)
    second(3)
    keep(1).start()
    update_second()

    for flow, q, targets, first_at in sent:

        def act(chunks, flow=flow, q=q, targets=targets, first_at=first_at):
            for i, to in enumerate(targets):
                pcopy(flow, q, to, first_at + i, chunks).wait_send()

        each_size(flow, q, act)
    for c, to, at in always:
        lcopy(c, to, at).wait_send()

    @pl.when(mid)
    def _():
        for c, to, at in middle:
            lcopy(c, to, at).wait_send()

    keep(0).wait()
    keep(1).wait()
    for i in range(4):
        stored(i).wait()


def shards(rhs_top, diag_inverse, panel_coupling, trailing_factor, rhs_trailing):
    anywhere = pl.BlockSpec(memory_space=pl.ANY)
    dma = pltpu.SemaphoreType.DMA
    return pl.pallas_call(
        kernel,
        out_shape=(
            jax.ShapeDtypeStruct((2, 32, 1024), BF),
            jax.ShapeDtypeStruct((1024, 1024), BF),
        ),
        in_specs=[pl.BlockSpec(memory_space=pltpu.HBM)] * 5,
        out_specs=(anywhere, anywhere),
        scratch_shapes=[
            pltpu.VMEM((3, 1024, 1024), BF),
            pltpu.VMEM((2, 4, 1024, 256), BF),
            pltpu.VMEM((2048, 1024), BF),
            pltpu.VMEM((1024, 1024), BF),
            pltpu.VMEM((16, 1024, 128), BF),
            pltpu.VMEM((1024, 1024), BF),
            pltpu.VMEM((1024, 1024), F32),
            pltpu.VMEM((1024, 1024), BF),
            dma((4, 32)),
            dma((16,)),
            dma((124,)),
            dma((17,)),
            dma((13,)),
            dma((2,)),
            dma((4,)),
        ],
        compiler_params=pltpu.CompilerParams(
            collective_id=0, has_side_effects=True, vmem_limit_bytes=50 * 1024 * 1024
        ),
        name="substitute",
    )(rhs_top, diag_inverse, panel_coupling, trailing_factor, rhs_trailing)


def solution(mesh):
    in_specs = (
        P(None, "row", "col"),
        P(None, "row", None),
        P("row", None),
        P("row", "col"),
        P("row", "col"),
    )
    out_specs = (P(None, "row", "col"), P("row", "col"))
    return jax.shard_map(shards, mesh=mesh, in_specs=in_specs, out_specs=out_specs, check_vma=False)
```
